512 devices in a mesh: sector: 64 (over x, z), mpo: 8 (over y, core).
Axes of the slice: x: 4, y: 4, z: 16, core: 2. Of those that a mesh axis runs over, the one named last changes fastest.
Arguments:
- wavefunction: bfloat16 [64, 512, 512], P('sector'), may hold values from -6 to 6
- left_environment: bfloat16 [32, 64, 512, 512], P('mpo', 'sector'), may hold values from -0.25 to 0.25
- right_environment: bfloat16 [32, 64, 512, 512], P('mpo', 'sector'), may hold values from -0.25 to 0.25
- term_shift: int32 [32], P('mpo'), may hold values from 0 to 4, as said below
- coupling: float32 [32], P('mpo'), may hold values from 0.1 to 0.4
- block_sizes: int32 [64], P('sector'), may hold values from 128 to 512
Outputs:
- applied: float32 [64, 512, 512], P('sector', 'mpo')
The draws below stay inside these ranges and needn't reach their ends.
Inputs may be any that keep to these rules, and one draw needn't show every extreme that they name: `term_shift`: each of the five codes is held by some MPO index.
All inputs are finite; a program needn't handle non-finite values.
Results may differ from the reference program's by a relative error of at most 0.0003.
Values may be sent and summed in bfloat16 or wider, within the bound.
No kernel may reach another device: no remote copies, remote signals or barrier semaphores. Data moves between devices by JAX's collectives and lax.ppermute only.
A program may use at most 64 MiB of HBM per device.

```python
import math
import jax
import jax.numpy as jnp
from jax import lax

BLOCK = 512
BOND = 32
GRID = 8
SECTORS = 64
N_SECTOR = 64


def draw_term_shift(key, part):
    order = jax.random.permutation(key, BOND)
    return (order % 5).astype(jnp.int32)


def plant(result, rng, least, largest):
    longest = result.shape.index(max(result.shape))
    spots = []
    for shift in (0, 1):
        where = [jax.random.randint(jax.random.fold_in(rng, axis), (), 0, length) for axis, length in enumerate(result.shape)]
        where[longest] = (where[longest] + shift) % result.shape[longest]
        spots.append(tuple(where))
    return result.at[spots[0]].set(least).at[spots[1]].set(largest)


def level_of(key, shape, split, low, top_value):
    loudness, own = 1.0, jax.random.fold_in(key, 6)
    for dim, parts in split:
        heights = jnp.exp(jax.random.uniform(jax.random.fold_in(own, dim), (parts,), jnp.float32, low / len(split), top_value / len(split)))
        loudness = loudness * jnp.repeat(heights, shape[dim] // parts).reshape([-1 if axis == dim else 1 for axis in range(len(shape))])
    return loudness


def bell_draw(stream_key, extent, spread, reach, pieces=(), dtype=jnp.bfloat16):
    values = jax.random.normal(stream_key, extent, jnp.float32) * spread
    if len(pieces) > 0:
        values = level_of(stream_key, extent, pieces, -0.22, 0.18) * values
    return jnp.clip(values, min=-reach, max=reach).astype(dtype)


def setup_inputs(seed: int = 0) -> dict:
    key_list = jax.random.split(jax.random.key(seed), 7)
    return {
        "wavefunction": bell_draw(key_list[0], (SECTORS, BLOCK, BLOCK), 1.0, 6.0, ((0, 64),)),
        "left_environment": bell_draw(key_list[1], (BOND, SECTORS, BLOCK, BLOCK), BLOCK ** -0.5, 0.25, ((0, 8), (1, 64))),
        "right_environment": bell_draw(key_list[2], (BOND, SECTORS, BLOCK, BLOCK), BLOCK ** -0.5, 0.25, ((0, 8), (1, 64))),
        "term_shift": draw_term_shift(jax.random.fold_in(key_list[6], 71), 0),
        "coupling": jnp.clip(jnp.exp(math.log(0.4) - 1.3862944 * jax.random.uniform(key_list[4], (BOND,), jnp.float32) ** level_of(key_list[4], (BOND,), ((0, 8),), -0.2, 0.2)), 0.1, 0.4),
        "block_sizes": plant(jax.random.randint(key_list[5], (SECTORS,), BLOCK // 4, BLOCK + 1), jax.random.fold_in(key_list[5], 1), BLOCK // 4, BLOCK).astype(jnp.int32),
    }


def reference(wavefunction, left_environment, right_environment, term_shift, coupling, block_sizes):
    positions = jnp.arange(BLOCK).astype(jnp.int32)
    live = positions[None, :] < block_sizes[:, None]
    block_mask = live[:, :, None] & live[:, None, :]
    masked = jnp.where(block_mask, wavefunction, jnp.zeros_like(wavefunction))
    sector = jnp.arange(N_SECTOR).astype(jnp.int32)

    def moved(offset):
        target = sector + offset
        valid = (target >= 0) & (target < N_SECTOR)
        source = jnp.clip(target, 0, N_SECTOR - 1)
        taken = jnp.take(masked, source, axis=0)
        return jnp.where(valid[:, None, None], taken, jnp.zeros_like(taken))

    candidates = jnp.stack([masked, moved(-1), moved(1), moved(-GRID), moved(GRID)])

    def one_sector(index):
        chosen = jnp.take(candidates[:, index], term_shift, axis=0)
        left = left_environment[:, index].astype(jnp.float32)
        partial_left = jnp.einsum("wij,wjk->wik", left, chosen.astype(jnp.float32), precision=lax.Precision.HIGHEST)
        products = jnp.einsum("wik,wlk->wil", partial_left, right_environment[:, index].astype(jnp.float32), precision=lax.Precision.HIGHEST)
        total = jnp.sum(coupling[:, None, None] * products, axis=0)
        return jnp.where(block_mask[index], total, jnp.zeros_like(total))

    return lax.map(one_sector, jnp.arange(N_SECTOR).astype(jnp.int32))
```

```python
import functools

import jax
import jax.numpy as jnp
from jax import lax
from jax.experimental import pallas as pl
from jax.experimental.pallas import tpu as pltpu
from jax.sharding import PartitionSpec as P

GRID = 8
CORES = 2


def terms_kernel(codes, first, last, shift, scale, size, parity, left, right, *rest):
    sources, rest = rest[: len(codes)], rest[len(codes) :]
    if not first:
        before, rest = rest[0], rest[1:]
    outs, rest = rest[: 2 if last else 1], rest[2 if last else 1 :]
    left_buf, right_buf, source_buf, acc, left_sem, right_sem, source_sem = rest[:7]
    count, extent = left.shape[0], left.shape[1]

    def wanted(w):
        return functools.reduce(jnp.logical_or, [shift[w] == code for code in codes])

    for w in range(count):
        @pl.when(wanted(w))
        def _():
            pltpu.make_async_copy(left.at[w], left_buf.at[w], left_sem.at[w]).start()
            pltpu.make_async_copy(right.at[w], right_buf.at[w], right_sem.at[w]).start()

        for code, source in zip(codes, sources):
            @pl.when(shift[w] == code)
            def _():
                pltpu.make_async_copy(source, source_buf.at[w], source_sem.at[w]).start()

    if first:
        acc[...] = jnp.zeros_like(acc)
    else:
        acc[...] = before[...]

    half = extent // 2

    @pl.loop(0, count)
    def _(w):
        @pl.when(wanted(w))
        def _():
            pltpu.make_async_copy(left.at[w], left_buf.at[w], left_sem.at[w]).wait()
            pltpu.make_async_copy(sources[0], source_buf.at[w], source_sem.at[w]).wait()
            pltpu.make_async_copy(right.at[w], right_buf.at[w], right_sem.at[w]).wait()
            for start in range(0, extent, half):
                rows = pl.ds(start, half)
                product = jnp.dot(
                    left_buf[w, rows, :], source_buf[w], preferred_element_type=jnp.float32
                )
                product = product * scale[w]
                high = product.astype(jnp.bfloat16)
                low = (product - high.astype(jnp.float32)).astype(jnp.bfloat16)
                along = (((1,), (1,)), ((), ()))
                total = lax.dot_general(
                    high, right_buf[w], along, preferred_element_type=jnp.float32
                )
                total += lax.dot_general(
                    low, right_buf[w], along, preferred_element_type=jnp.float32
                )
                acc[rows, :] += total

    if not last:
        outs[0][...] = acc[...]
        return
    kept, given = outs
    step = extent // (kept.shape[0] * CORES)
    for piece in range(kept.shape[0] * CORES):
        rows = pl.ds(piece * step, step)
        at = (piece * step + lax.broadcasted_iota(jnp.int32, (step, extent), 0)) < size[0]
        at &= lax.broadcasted_iota(jnp.int32, (step, extent), 1) < size[0]
        value = jnp.where(at, acc[rows, :], 0.0)

        @pl.when(parity[0] == piece % CORES)
        def _():
            kept[piece // CORES] = value

        @pl.when(parity[0] != piece % CORES)
        def _():
            given[piece // CORES] = value


def terms(codes, sources, before, last, shift, scale, size, parity, left, right, chips):
    count, extent = left.shape[0], left.shape[1]
    first = before is None
    smem = pl.BlockSpec(memory_space=pltpu.SMEM)
    vmem = pl.BlockSpec(memory_space=pltpu.VMEM)
    anywhere = pl.BlockSpec(memory_space=pl.ANY)
    if last:
        piece = jax.ShapeDtypeStruct((chips, extent // (chips * CORES), extent), jnp.float32)
        out_shape, out_specs = (piece, piece), (vmem, vmem)
    else:
        out_shape, out_specs = jax.ShapeDtypeStruct((extent, extent), jnp.float32), vmem
    return pl.pallas_call(
        functools.partial(terms_kernel, codes, first, last),
        out_shape=out_shape,
        in_specs=[smem] * 4 + [anywhere] * (2 + len(sources)) + ([] if first else [vmem]),
        out_specs=out_specs,
        scratch_shapes=[
            pltpu.VMEM((count, extent, extent), jnp.bfloat16),
            pltpu.VMEM((count, extent, extent), jnp.bfloat16),
            pltpu.VMEM((count, extent, extent), jnp.bfloat16),
            pltpu.VMEM((extent, extent), jnp.float32),
            pltpu.SemaphoreType.DMA((count,)),
            pltpu.SemaphoreType.DMA((count,)),
            pltpu.SemaphoreType.DMA((count,)),
        ],
        compiler_params=pltpu.CompilerParams(vmem_limit_bytes=24 << 20),
        cost_estimate=pl.CostEstimate(
            flops=count * extent**3 * 3, bytes_accessed=count * extent**2 * 4, transcendentals=0
        ),
    )(shift, scale, size, parity, left, right, *sources, *([] if first else [before]))


def per_device(
    wavefunction, left_environment, right_environment, term_shift, coupling, block_sizes
):
    extent = wavefunction.shape[1]
    sectors, members = lax.axis_size("sector"), lax.axis_size("mpo")
    chips = members // CORES
    me = lax.axis_index("mpo")
    chip, parity = me // CORES, me % CORES
    both = ("sector", "mpo")
    same_core = [[y * CORES + c for y in range(chips)] for c in range(CORES)]
    swap = [(m, m ^ 1) for m in range(members)]

    def route(distance):
        pairs = []
        for s in range(sectors):
            for m in range(members):
                source = s + distance if m % CORES == 0 else s - distance
                if 0 <= source < sectors:
                    pairs.append((source * members + m, s * members + m))
        return pairs

    positions = jnp.arange(extent)
    live = positions < block_sizes[0]
    masked = jnp.where(live[:, None] & live[None, :], wavefunction[0], 0)
    share = extent // chips
    strip = lax.dynamic_slice_in_dim(masked, chip * share, share, 0)

    near_one = lax.ppermute(masked, both, route(1))
    far_strip = lax.ppermute(strip, both, route(GRID))
    near_two = lax.ppermute(near_one, "mpo", swap)
    left = left_environment[:, 0]
    right = right_environment[:, 0]
    is_first = parity == 0
    table = jnp.where(
        is_first, jnp.array([0, 2, 1, 4, 3], jnp.int32), jnp.array([0, 1, 2, 3, 4], jnp.int32)
    )
    shift = jnp.sum(jnp.where(term_shift[:, None] == jnp.arange(5)[None], table[None], 0), axis=1)
    shift = shift.astype(jnp.int32)
    par = parity[None].astype(jnp.int32)
    shared = (shift, coupling, block_sizes, par, left, right, chips)
    early = terms((0, 1, 2), (masked, near_one, near_two), None, False, *shared)

    spread = jnp.broadcast_to(far_strip[None], (chips,) + far_strip.shape)
    far_one = lax.all_to_all(spread, "mpo", 0, 0, axis_index_groups=same_core)
    far_one = far_one.reshape(extent, extent)
    far_two = lax.ppermute(far_one, "mpo", swap)
    kept, given = terms((3, 4), (far_one, far_two), early, True, *shared)

    half = kept + lax.ppermute(given, "mpo", swap)
    pieces = lax.all_to_all(half, "mpo", 0, 0, axis_index_groups=same_core)
    return jnp.sum(pieces, axis=0)[None]


def solution(mesh):
    placed = (
        P("sector", None, None),
        P("mpo", "sector", None, None),
        P("mpo", "sector", None, None),
        P("mpo"),
        P("mpo"),
        P("sector"),
    )
    return jax.shard_map(
        per_device, mesh=mesh, in_specs=placed, out_specs=P("sector", "mpo", None), check_vma=False
    )
```

```python
import functools

import jax
import jax.numpy as jnp
from jax import lax
from jax.experimental import pallas as pl
from jax.experimental.pallas import tpu as pltpu
from jax.sharding import PartitionSpec as P


GRID = 8
CORES = 2
NEAR = ((2.0, 1.0), (1.0, 2.0))
FAR = ((4.0, 3.0), (3.0, 4.0))


def terms_kernel(early, size, parity, mine, other, *rest):
    lefts, rights, rest = rest[0:2], rest[2:4], rest[4:]
    n = 3 if early else 2
    sources, rest = rest[:n], rest[n:]
    if not early:
        before, rest = rest[0], rest[1:]
    out, left_buf, right_buf, acc, left_sem, right_sem = rest
    count, chips, step, extent = left_buf.shape[0] // 2, *left_buf.shape[1:]
    core = parity[0]

    def code(w):
        return jnp.where(w < count, mine[w % count], other[w % count])

    def uses(w, source):
        if early and source == 0:
            return code(w) == 0.0
        table = (NEAR if early else FAR)[source - 1 if early else source]
        return code(w) == jnp.where(core == 0, table[0], table[1])

    def fetch_left(w, k):
        return pltpu.make_async_copy(lefts[k].at[w % count, :, core], left_buf.at[w], left_sem.at[w])

    def fetch_right(w, k):
        return pltpu.make_async_copy(rights[k].at[w % count], right_buf.at[w], right_sem.at[w])

    for k in range(n):
        for w in range(2 * count):
            @pl.when(uses(w, k))
            def _():
                fetch_left(w, w // count).start()
                fetch_right(w, w // count).start()

    if early:
        acc[...] = jnp.zeros_like(acc)
    else:
        acc[...] = before[...]

    for k in range(n):
        @pl.loop(0, 2 * count)
        def _(w):
            @pl.when(uses(w, k))
            def _():
                fetch_left(w, 0).wait()
                product = jnp.dot(
                    left_buf[w].reshape(chips * step, extent),
                    sources[k][...],
                    preferred_element_type=jnp.float32,
                )
                scale = jnp.where(w < count, mine[count + w % count], other[count + w % count])
                product = product * scale
                high = product.astype(jnp.bfloat16)
                low = (product - high.astype(jnp.float32)).astype(jnp.bfloat16)
                fetch_right(w, 0).wait()
                along = (((1,), (1,)), ((), ()))
                total = lax.dot_general(
                    high, right_buf[w], along, preferred_element_type=jnp.float32
                )
                total += lax.dot_general(
                    low, right_buf[w], along, preferred_element_type=jnp.float32
                )
                acc[...] += total

    if early:
        out[...] = acc[...]
        return
    for y in range(chips):
        row = (y * CORES + core) * step + lax.broadcasted_iota(jnp.int32, (step, extent), 0)
        column = lax.broadcasted_iota(jnp.int32, (step, extent), 1)
        live = (row < size[0]) & (column < size[0])
        out[y] = jnp.where(live, acc[pl.ds(y * step, step), :], 0.0)


def terms(sources, before, size, parity, mine, other, lefts, rights):
    early = before is None
    count, chips, _, step, extent = lefts[0].shape
    smem = pl.BlockSpec(memory_space=pltpu.SMEM)
    vmem = pl.BlockSpec(memory_space=pltpu.VMEM)
    anywhere = pl.BlockSpec(memory_space=pl.ANY)
    shape = (chips * step, extent) if early else (chips, step, extent)
    held = sources if early else (*sources, before)
    held = [pltpu.with_memory_space_constraint(a, pltpu.VMEM) for a in held]
    return pl.pallas_call(
        functools.partial(terms_kernel, early),
        out_shape=jax.ShapeDtypeStruct(shape, jnp.float32),
        in_specs=[smem] * 4 + [anywhere] * 4 + [vmem] * len(held),
        out_specs=vmem,
        scratch_shapes=[
            pltpu.VMEM((2 * count, chips, step, extent), jnp.bfloat16),
            pltpu.VMEM((2 * count, extent, extent), jnp.bfloat16),
            pltpu.VMEM((chips * step, extent), jnp.float32),
            pltpu.SemaphoreType.DMA((2 * count,)),
            pltpu.SemaphoreType.DMA((2 * count,)),
        ],
        compiler_params=pltpu.CompilerParams(vmem_limit_bytes=16 << 20),
        cost_estimate=pl.CostEstimate(
            flops=count * extent**3 * 3, bytes_accessed=count * extent**2 * 4, transcendentals=0
        ),
    )(size, parity, mine, other, *lefts, *rights, *held)


def per_device(
    wavefunction, left_environment, right_environment, term_shift, coupling, block_sizes
):
    extent = wavefunction.shape[1]
    sectors, members = lax.axis_size("sector"), lax.axis_size("mpo")
    chips = members // CORES
    step = extent // members
    me = lax.axis_index("mpo")
    chip, parity = me // CORES, me % CORES
    both = ("sector", "mpo")
    same_core = [[y * CORES + c for y in range(chips)] for c in range(CORES)]
    swap = [(m, m ^ 1) for m in range(members)]

    def route(source_of):
        pairs = []
        for s in range(sectors):
            for m in range(members):
                source, core = source_of(s, m % CORES)
                if 0 <= source < sectors:
                    pairs.append((source * members + m - m % CORES + core, s * members + m))
        return pairs

    late = lambda s: s % (2 * GRID) >= GRID
    nowhere = (-1, 0)
    near = route(lambda s, c: (s + 1, 0) if c == 0 else (s - 1, 1))
    far_above = route(lambda s, c: (s + GRID, 0) if c == 0 else nowhere)
    far_below = route(
        lambda s, c: nowhere if c == 0 else (s - GRID, 0 if late(s - GRID) else 1)
    )

    size = block_sizes[0]
    positions = jnp.arange(extent)
    share = extent // chips
    strip = lax.dynamic_slice_in_dim(wavefunction[0], chip * share, share, 0)
    rows = chip * share + jnp.arange(share)
    strip = jnp.where((rows < size)[:, None] & (positions < size)[None, :], strip, 0)
    above_strip = lax.ppermute(strip, both, far_above)
    below_strip = lax.ppermute(strip, both, far_below)
    live = positions < size
    masked = jnp.where(live[:, None] & live[None, :], wavefunction[0], 0)
    near_one = lax.ppermute(masked, both, near)

    in_hbm = lambda a: pltpu.with_memory_space_constraint(a, pltpu.HBM)
    by_core = lambda a: in_hbm(a.reshape(a.shape[0], chips, CORES, step, extent))
    left, right = left_environment[:, 0], right_environment[:, 0]
    mine = jnp.concatenate([term_shift.astype(jnp.float32), coupling])
    right_other = lax.ppermute(right, "mpo", swap)
    left_other = lax.ppermute(left, "mpo", swap)
    other = lax.ppermute(mine, "mpo", swap)
    near_two = lax.ppermute(near_one, "mpo", swap)
    lefts = (by_core(left), by_core(left_other))
    rights = (in_hbm(right), in_hbm(right_other))
    shared = (block_sizes, parity[None].astype(jnp.int32), mine, other, lefts, rights)

    far_strip = jnp.where(parity == 0, above_strip, below_strip)
    spread = jnp.broadcast_to(far_strip[None], (chips,) + far_strip.shape)
    far_one = lax.all_to_all(spread, "mpo", 0, 0, axis_index_groups=same_core)
    far_one = far_one.reshape(extent, extent)
    early = terms((masked, near_one, near_two), None, *shared)
    far_two = lax.ppermute(far_one, "mpo", swap)
    half = terms((far_one, far_two), early, *shared)
    pieces = lax.all_to_all(half, "mpo", 0, 0, axis_index_groups=same_core)
    return jnp.sum(pieces, axis=0)[None]


def solution(mesh):
    placed = (
        P("sector", None, None),
        P("mpo", "sector", None, None),
        P("mpo", "sector", None, None),
        P("mpo"),
        P("mpo"),
        P("sector"),
    )

    return jax.shard_map(
        per_device, mesh=mesh, in_specs=placed, out_specs=P("sector", "mpo", None), check_vma=False
    )
```

```python
import functools

import jax
import jax.numpy as jnp
from jax import lax
from jax.experimental import pallas as pl
from jax.experimental.pallas import tpu as pltpu
from jax.sharding import PartitionSpec as P


GRID = 8
CORES = 2
EARLY = ((0.0, 0.0), (2.0, 1.0), (1.0, 2.0))
LATE = ((4.0, 3.0), (3.0, 4.0))


def terms_kernel(early, size, parity, mine, other, *rest):
    lefts, rights, rest = rest[0:2], rest[2:4], rest[4:]
    codes = EARLY if early else LATE
    n = len(codes)
    sources, rest = rest[:n], rest[n:]
    if not early:
        before, rest = rest[0], rest[1:]
    out, left_buf, right_buf, acc, scale, sems = rest
    count, (chips, step, extent) = left_buf.shape[0] // 2, left_buf.shape[1:]
    core = parity[0]

    def fetch_left(k, w, at):
        return pltpu.make_async_copy(lefts[k].at[w, :, core], left_buf.at[at], sems.at[0, at])

    def fetch_right(k, w, at):
        return pltpu.make_async_copy(rights[k].at[w], right_buf.at[at], sems.at[1, at])

    found, begins = jnp.int32(0), []
    for on_core in codes:
        begins.append(found)
        for k, facts in enumerate((mine, other)):
            for w in range(count):
                takes = facts[w] == jnp.where(core == 0, *on_core)

                @pl.when(takes)
                def _(found=found):
                    fetch_left(k, w, found).start()
                    fetch_right(k, w, found).start()
                    scale[found] = facts[count + w]

                found += takes.astype(jnp.int32)
    begins.append(found)

    if early:
        acc[...] = jnp.zeros_like(acc)
    else:
        acc[...] = before[...]

    along = (((1,), (1,)), ((), ()))

    def add(source, slots):
        parts = []
        for at in slots:
            fetch_left(0, 0, at).wait()
            rows = left_buf[at].reshape(chips * step, extent)
            product = jnp.dot(rows, source[...], preferred_element_type=jnp.float32) * scale[at]
            high = product.astype(jnp.bfloat16)
            low = (product - high.astype(jnp.float32)).astype(jnp.bfloat16)
            parts.append((high, low))
        total = acc[...]
        for at, (high, low) in zip(slots, parts):
            fetch_right(0, 0, at).wait()
            right = right_buf[at]
            total += lax.dot_general(high, right, along, preferred_element_type=jnp.float32)
            total += lax.dot_general(low, right, along, preferred_element_type=jnp.float32)
        acc[...] = total

    for source, begin, end in zip(sources, begins, begins[1:]):
        @pl.loop(0, (end - begin) >> 1)
        def _(pair):
            add(source, (begin + 2 * pair, begin + 2 * pair + 1))

        @pl.when(((end - begin) & 1) == 1)
        def _():
            add(source, (end - 1,))

    if early:
        out[...] = acc[...]
        return
    for y in range(chips):
        row = (y * CORES + core) * step + lax.broadcasted_iota(jnp.int32, (step, extent), 0)
        column = lax.broadcasted_iota(jnp.int32, (step, extent), 1)
        live = (row < size[0]) & (column < size[0])
        out[y] = jnp.where(live, acc[pl.ds(y * step, step), :], 0.0)


def terms(sources, before, size, parity, mine, other, lefts, rights):
    early = before is None
    count, chips, _, step, extent = lefts[0].shape
    smem = pl.BlockSpec(memory_space=pltpu.SMEM)
    vmem = pl.BlockSpec(memory_space=pltpu.VMEM)
    anywhere = pl.BlockSpec(memory_space=pl.ANY)
    shape = (chips * step, extent) if early else (chips, step, extent)
    held = sources if early else (*sources, before)
    held = [pltpu.with_memory_space_constraint(a, pltpu.VMEM) for a in held]
    return pl.pallas_call(
        functools.partial(terms_kernel, early),
        out_shape=jax.ShapeDtypeStruct(shape, jnp.float32),
        in_specs=[smem] * 4 + [anywhere] * 4 + [vmem] * len(held),
        out_specs=vmem,
        scratch_shapes=[
            pltpu.VMEM((2 * count, chips, step, extent), jnp.bfloat16),
            pltpu.VMEM((2 * count, extent, extent), jnp.bfloat16),
            pltpu.VMEM((chips * step, extent), jnp.float32),
            pltpu.SMEM((2 * count,), jnp.float32),
            pltpu.SemaphoreType.DMA((2, 2 * count)),
        ],
        compiler_params=pltpu.CompilerParams(vmem_limit_bytes=16 << 20),
        cost_estimate=pl.CostEstimate(
            flops=count * extent**3 * 3, bytes_accessed=count * extent**2 * 4, transcendentals=0
        ),
    )(size, parity, mine, other, *lefts, *rights, *held)


def per_device(
    wavefunction, left_environment, right_environment, term_shift, coupling, block_sizes
):
    extent = wavefunction.shape[1]
    sectors, members = lax.axis_size("sector"), lax.axis_size("mpo")
    chips = members // CORES
    step = extent // members
    me = lax.axis_index("mpo")
    chip, parity = me // CORES, me % CORES
    both = ("sector", "mpo")
    same_core = [[y * CORES + c for y in range(chips)] for c in range(CORES)]
    swap = [(m, m ^ 1) for m in range(members)]

    def route(source_of):
        pairs = []
        for s in range(sectors):
            for m in range(members):
                source, core = source_of(s, m % CORES)
                if 0 <= source < sectors:
                    pairs.append((source * members + m - m % CORES + core, s * members + m))
        return pairs

    late = lambda s: s % (2 * GRID) >= GRID
    nowhere = (-1, 0)
    near = route(lambda s, c: (s + 1, 0) if c == 0 else (s - 1, 1))
    far_above = route(lambda s, c: (s + GRID, 0) if c == 0 else nowhere)
    far_below = route(
        lambda s, c: nowhere if c == 0 else (s - GRID, 0 if late(s - GRID) else 1)
    )

    size = block_sizes[0]
    positions = jnp.arange(extent)
    share = extent // chips
    strip = lax.dynamic_slice_in_dim(wavefunction[0], chip * share, share, 0)
    rows = chip * share + jnp.arange(share)
    strip = jnp.where((rows < size)[:, None] & (positions < size)[None, :], strip, 0)
    above_strip = lax.ppermute(strip, both, far_above)
    below_strip = lax.ppermute(strip, both, far_below)
    live = positions < size
    masked = jnp.where(live[:, None] & live[None, :], wavefunction[0], 0)
    near_one = lax.ppermute(masked, both, near)

    in_hbm = lambda a: pltpu.with_memory_space_constraint(a, pltpu.HBM)
    by_core = lambda a: in_hbm(a.reshape(a.shape[0], chips, CORES, step, extent))
    left, right = left_environment[:, 0], right_environment[:, 0]
    count = coupling.shape[0]
    mine = jnp.where(
        jnp.arange(2 * count) < count,
        jnp.pad(term_shift, (0, count)).astype(jnp.float32),
        jnp.pad(coupling, (count, 0)),
    )
    right_other = lax.ppermute(right, "mpo", swap)
    left_other = lax.ppermute(left, "mpo", swap)
    other = lax.ppermute(mine, "mpo", swap)
    near_two = lax.ppermute(near_one, "mpo", swap)
    lefts = (by_core(left), by_core(left_other))
    rights = (in_hbm(right), in_hbm(right_other))
    shared = (block_sizes, parity[None].astype(jnp.int32), mine, other, lefts, rights)

    far_strip = jnp.where(parity == 0, above_strip, below_strip)
    spread = jnp.broadcast_to(far_strip[None], (chips,) + far_strip.shape)
    far_one = lax.all_to_all(spread, "mpo", 0, 0, axis_index_groups=same_core)
    far_one = far_one.reshape(extent, extent)
    early = terms((masked, near_one, near_two), None, *shared)
    far_two = lax.ppermute(far_one, "mpo", swap)
    half = terms((far_one, far_two), early, *shared)
    pieces = lax.all_to_all(half, "mpo", 0, 0, axis_index_groups=same_core)
    return jnp.sum(pieces, axis=0)[None]


def solution(mesh):
    placed = (
        P("sector", None, None),
        P("mpo", "sector", None, None),
        P("mpo", "sector", None, None),
        P("mpo"),
        P("mpo"),
        P("sector"),
    )

    return jax.shard_map(
        per_device, mesh=mesh, in_specs=placed, out_specs=P("sector", "mpo", None), check_vma=False
    )
```

```python
import functools
import math

import jax
import jax.numpy as jnp
from jax import lax
from jax.experimental import pallas as pl
from jax.experimental.pallas import tpu as pltpu
from jax.sharding import PartitionSpec as P


GRID = 8
CORES = 2
TOP = 14.0
NOTE = 8
EARLY = ((0.0, 0.0), (2.0, 1.0), (1.0, 2.0))
LATE = ((4.0, 3.0), (3.0, 4.0))


def terms_kernel(early, size, parity, mine, other, *rest):
    lefts, rights, rest = rest[0:2], rest[2:4], rest[4:]
    codes = EARLY if early else LATE
    n = len(codes)
    sources, rest = rest[:n], rest[n:]
    if not early:
        before, rest = rest[0], rest[1:]
    out, left_buf, right_buf, acc, scale, sems = rest
    count, (chips, step, extent) = left_buf.shape[0] // 2, left_buf.shape[1:]
    core = parity[0]

    def fetch_left(k, w, at):
        return pltpu.make_async_copy(lefts[k].at[w, :, core], left_buf.at[at], sems.at[0, at])

    def fetch_right(k, w, at):
        return pltpu.make_async_copy(rights[k].at[w], right_buf.at[at], sems.at[1, at])

    found, begins = jnp.int32(0), []
    for on_core in codes:
        begins.append(found)
        for k, facts in enumerate((mine, other)):
            for w in range(count):
                takes = facts[w] == jnp.where(core == 0, *on_core)

                @pl.when(takes)
                def _(found=found):
                    fetch_left(k, w, found).start()
                    fetch_right(k, w, found).start()
                    scale[found] = facts[count + w]

                found += takes.astype(jnp.int32)
    begins.append(found)

    if early:
        acc[...] = jnp.zeros_like(acc)
    else:
        acc[...] = before[...]

    along = (((1,), (1,)), ((), ()))

    def add(source, slots):
        parts = []
        for at in slots:
            fetch_left(0, 0, at).wait()
            rows = left_buf[at].reshape(chips * step, extent)
            product = jnp.dot(rows, source[...], preferred_element_type=jnp.float32) * scale[at]
            high = product.astype(jnp.bfloat16)
            low = (product - high.astype(jnp.float32)).astype(jnp.bfloat16)
            parts.append((high, low))
        total = acc[...]
        for at, (high, low) in zip(slots, parts):
            fetch_right(0, 0, at).wait()
            right = right_buf[at]
            total += lax.dot_general(high, right, along, preferred_element_type=jnp.float32)
            total += lax.dot_general(low, right, along, preferred_element_type=jnp.float32)
        acc[...] = total

    for source, begin, end in zip(sources, begins, begins[1:]):
        @pl.loop(0, (end - begin) >> 1)
        def _(pair):
            add(source, (begin + 2 * pair, begin + 2 * pair + 1))

        @pl.when(((end - begin) & 1) == 1)
        def _():
            add(source, (end - 1,))

    if early:
        out[...] = acc[...]
        return
    largest = jnp.zeros((1, 1), jnp.float32)
    for y in range(chips):
        row = (y * CORES + core) * step + lax.broadcasted_iota(jnp.int32, (step, extent), 0)
        column = lax.broadcasted_iota(jnp.int32, (step, extent), 1)
        live = (row < size[0]) & (column < size[0])
        rows = pl.ds(y * step, step)
        value = jnp.where(live, acc[rows, :], 0.0)
        acc[rows, :] = value
        largest = jnp.maximum(largest, jnp.max(jnp.abs(value), axis=(0, 1), keepdims=True))
    exponent = jnp.ceil(jnp.log(jnp.maximum(largest, 1e-30)) * (1 / math.log(2)))
    factor = jnp.exp2(TOP - exponent)
    for y in range(chips):
        out[y, pl.ds(0, step), :] = acc[pl.ds(y * step, step), :] * factor
        out[y, pl.ds(step, NOTE), :] = jnp.broadcast_to(exponent, (NOTE, extent))


def terms(sources, before, size, parity, mine, other, lefts, rights):
    early = before is None
    count, chips, _, step, extent = lefts[0].shape
    smem = pl.BlockSpec(memory_space=pltpu.SMEM)
    vmem = pl.BlockSpec(memory_space=pltpu.VMEM)
    anywhere = pl.BlockSpec(memory_space=pl.ANY)
    shape = (chips * step, extent) if early else (chips, step + NOTE, extent)
    held = sources if early else (*sources, before)
    held = [pltpu.with_memory_space_constraint(a, pltpu.VMEM) for a in held]
    return pl.pallas_call(
        functools.partial(terms_kernel, early),
        out_shape=jax.ShapeDtypeStruct(shape, jnp.float32),
        in_specs=[smem] * 4 + [anywhere] * 4 + [vmem] * len(held),
        out_specs=vmem,
        scratch_shapes=[
            pltpu.VMEM((2 * count, chips, step, extent), jnp.bfloat16),
            pltpu.VMEM((2 * count, extent, extent), jnp.bfloat16),
            pltpu.VMEM((chips * step, extent), jnp.float32),
            pltpu.SMEM((2 * count,), jnp.float32),
            pltpu.SemaphoreType.DMA((2, 2 * count)),
        ],
        compiler_params=pltpu.CompilerParams(vmem_limit_bytes=16 << 20),
        cost_estimate=pl.CostEstimate(
            flops=count * extent**3 * 3, bytes_accessed=count * extent**2 * 4, transcendentals=0
        ),
    )(size, parity, mine, other, *lefts, *rights, *held)


def per_device(
    wavefunction, left_environment, right_environment, term_shift, coupling, block_sizes
):
    extent = wavefunction.shape[1]
    sectors, members = lax.axis_size("sector"), lax.axis_size("mpo")
    chips = members // CORES
    step = extent // members
    me = lax.axis_index("mpo")
    chip, parity = me // CORES, me % CORES
    both = ("sector", "mpo")
    same_core = [[y * CORES + c for y in range(chips)] for c in range(CORES)]
    swap = [(m, m ^ 1) for m in range(members)]

    def route(source_of):
        pairs = []
        for s in range(sectors):
            for m in range(members):
                source, core = source_of(s, m % CORES)
                if 0 <= source < sectors:
                    pairs.append((source * members + m - m % CORES + core, s * members + m))
        return pairs

    late = lambda s: s % (2 * GRID) >= GRID
    nowhere = (-1, 0)
    near = route(lambda s, c: (s + 1, 0) if c == 0 else (s - 1, 1))
    far_above = route(lambda s, c: (s + GRID, 0) if c == 0 else nowhere)
    far_below = route(
        lambda s, c: nowhere if c == 0 else (s - GRID, 0 if late(s - GRID) else 1)
    )

    size = block_sizes[0]
    positions = jnp.arange(extent)
    share = extent // chips
    strip = lax.dynamic_slice_in_dim(wavefunction[0], chip * share, share, 0)
    rows = chip * share + jnp.arange(share)
    strip = jnp.where((rows < size)[:, None] & (positions < size)[None, :], strip, 0)
    above_strip = lax.ppermute(strip, both, far_above)
    below_strip = lax.ppermute(strip, both, far_below)
    live = positions < size
    masked = jnp.where(live[:, None] & live[None, :], wavefunction[0], 0)
    near_one = lax.ppermute(masked, both, near)

    in_hbm = lambda a: pltpu.with_memory_space_constraint(a, pltpu.HBM)
    by_core = lambda a: in_hbm(a.reshape(a.shape[0], chips, CORES, step, extent))
    left, right = left_environment[:, 0], right_environment[:, 0]
    count = coupling.shape[0]
    mine = jnp.where(
        jnp.arange(2 * count) < count,
        jnp.pad(term_shift, (0, count)).astype(jnp.float32),
        jnp.pad(coupling, (count, 0)),
    )
    right_other = lax.ppermute(right, "mpo", swap)
    left_other = lax.ppermute(left, "mpo", swap)
    other = lax.ppermute(mine, "mpo", swap)
    near_two = lax.ppermute(near_one, "mpo", swap)
    lefts = (by_core(left), by_core(left_other))
    rights = (in_hbm(right), in_hbm(right_other))
    shared = (block_sizes, parity[None].astype(jnp.int32), mine, other, lefts, rights)

    far_strip = jnp.where(parity == 0, above_strip, below_strip)
    spread = jnp.broadcast_to(far_strip[None], (chips,) + far_strip.shape)
    far_one = lax.all_to_all(spread, "mpo", 0, 0, axis_index_groups=same_core)
    far_one = far_one.reshape(extent, extent)
    early = terms((masked, near_one, near_two), None, *shared)
    far_two = lax.ppermute(far_one, "mpo", swap)
    half = terms((far_one, far_two), early, *shared)
    half = half.astype(jnp.float16)
    pieces = lax.all_to_all(half, "mpo", 0, 0, axis_index_groups=same_core)
    pieces = pieces.astype(jnp.float32)
    factor = jnp.exp2(pieces[:, step : step + 1] - TOP)
    return jnp.sum(pieces[:, :step] * factor, axis=0)[None]


def solution(mesh):
    placed = (
        P("sector", None, None),
        P("mpo", "sector", None, None),
        P("mpo", "sector", None, None),
        P("mpo"),
        P("mpo"),
        P("sector"),
    )

    return jax.shard_map(
        per_device, mesh=mesh, in_specs=placed, out_specs=P("sector", "mpo", None), check_vma=False
    )
```

```python
import functools
import math

import jax
import jax.numpy as jnp
from jax import lax
from jax.experimental import pallas as pl
from jax.experimental.pallas import tpu as pltpu
from jax.sharding import PartitionSpec as P


GRID = 8
CORES = 2
TOP = 14.0
NOTE = 8
EARLY = ((0.0, 0.0), (2.0, 1.0), (1.0, 2.0))
LATE = ((4.0, 3.0), (3.0, 4.0))


def terms_kernel(early, mine, other, *rest):
    lefts, rights, rest = rest[0:2], rest[2:4], rest[4:]
    codes = EARLY if early else LATE
    n = len(codes)
    sources, rest = rest[:n], rest[n:]
    if not early:
        before, rest = rest[0], rest[1:]
    out, left_buf, right_buf, scale, sems, *rest = rest
    acc = out if early else rest[0]
    count, (chips, step, extent) = left_buf.shape[0] // 2, left_buf.shape[1:]
    core, size = mine[2 * count].astype(jnp.int32), mine[2 * count + 1].astype(jnp.int32)

    def fetch_left(k, w, at):
        return pltpu.make_async_copy(lefts[k].at[w, :, core], left_buf.at[at], sems.at[0, at])

    def fetch_right(k, w, at):
        return pltpu.make_async_copy(rights[k].at[w], right_buf.at[at], sems.at[1, at])

    found, begins = jnp.int32(0), []
    for on_core in codes:
        begins.append(found)
        for k, facts in enumerate((mine, other)):
            for w in range(count):
                takes = facts[w] == jnp.where(core == 0, *on_core)

                @pl.when(takes)
                def _(found=found):
                    fetch_left(k, w, found).start()
                    fetch_right(k, w, found).start()
                    scale[found] = facts[count + w]

                found += takes.astype(jnp.int32)
    begins.append(found)

    if early:
        acc[...] = jnp.zeros_like(acc)
    else:
        acc[...] = before[...]

    along = (((1,), (1,)), ((), ()))

    def add(source, slots):
        parts = []
        for at in slots:
            fetch_left(0, 0, at).wait()
            rows = left_buf[at].reshape(chips * step, extent)
            product = jnp.dot(rows, source[...], preferred_element_type=jnp.float32) * scale[at]
            high = product.astype(jnp.bfloat16)
            low = (product - high.astype(jnp.float32)).astype(jnp.bfloat16)
            parts.append((high, low))
        total = acc[...]
        for at, (high, low) in zip(slots, parts):
            fetch_right(0, 0, at).wait()
            right = right_buf[at]
            total += lax.dot_general(high, right, along, preferred_element_type=jnp.float32)
            total += lax.dot_general(low, right, along, preferred_element_type=jnp.float32)
        acc[...] = total

    for source, begin, end in zip(sources, begins, begins[1:]):
        @pl.loop(0, (end - begin) >> 1)
        def _(pair):
            add(source, (begin + 2 * pair, begin + 2 * pair + 1))

        @pl.when(((end - begin) & 1) == 1)
        def _():
            add(source, (end - 1,))

    if early:
        return
    largest = jnp.zeros((1, 1), jnp.float32)
    for y in range(chips):
        row = (y * CORES + core) * step + lax.broadcasted_iota(jnp.int32, (step, extent), 0)
        column = lax.broadcasted_iota(jnp.int32, (step, extent), 1)
        live = (row < size) & (column < size)
        rows = pl.ds(y * step, step)
        value = jnp.where(live, acc[rows, :], 0.0)
        acc[rows, :] = value
        largest = jnp.maximum(largest, jnp.max(jnp.abs(value), axis=(0, 1), keepdims=True))
    exponent = jnp.ceil(jnp.log(jnp.maximum(largest, 1e-30)) * (1 / math.log(2)))
    factor = jnp.exp2(TOP - exponent)
    for y in range(chips):
        out[y, pl.ds(0, step), :] = acc[pl.ds(y * step, step), :] * factor
        out[y, pl.ds(step, NOTE), :] = jnp.broadcast_to(exponent, (NOTE, extent))


def terms(sources, before, mine, other, lefts, rights):
    early = before is None
    count, chips, _, step, extent = lefts[0].shape
    smem = pl.BlockSpec(memory_space=pltpu.SMEM)
    vmem = pl.BlockSpec(memory_space=pltpu.VMEM)
    anywhere = pl.BlockSpec(memory_space=pl.ANY)
    shape = (chips * step, extent) if early else (chips, step + NOTE, extent)
    held = sources if early else (*sources, before)
    held = [pltpu.with_memory_space_constraint(a, pltpu.VMEM) for a in held]
    return pl.pallas_call(
        functools.partial(terms_kernel, early),
        out_shape=jax.ShapeDtypeStruct(shape, jnp.float32),
        in_specs=[smem] * 2 + [anywhere] * 4 + [vmem] * len(held),
        out_specs=vmem,
        scratch_shapes=[
            pltpu.VMEM((2 * count, chips, step, extent), jnp.bfloat16),
            pltpu.VMEM((2 * count, extent, extent), jnp.bfloat16),
            pltpu.SMEM((2 * count,), jnp.float32),
            pltpu.SemaphoreType.DMA((2, 2 * count)),
        ]
        + ([] if early else [pltpu.VMEM((chips * step, extent), jnp.float32)]),
        compiler_params=pltpu.CompilerParams(vmem_limit_bytes=16 << 20),
        cost_estimate=pl.CostEstimate(
            flops=count * extent**3 * 3, bytes_accessed=count * extent**2 * 4, transcendentals=0
        ),
    )(mine, other, *lefts, *rights, *held)


def per_device(
    wavefunction, left_environment, right_environment, term_shift, coupling, block_sizes
):
    extent = wavefunction.shape[1]
    sectors, members = lax.axis_size("sector"), lax.axis_size("mpo")
    chips = members // CORES
    step = extent // members
    me = lax.axis_index("mpo")
    chip, parity = me // CORES, me % CORES
    both = ("sector", "mpo")
    same_core = [[y * CORES + c for y in range(chips)] for c in range(CORES)]
    swap = [(m, m ^ 1) for m in range(members)]

    def route(source_of):
        pairs = []
        for s in range(sectors):
            for m in range(members):
                source, core = source_of(s, m % CORES)
                if 0 <= source < sectors:
                    pairs.append((source * members + m - m % CORES + core, s * members + m))
        return pairs

    late = lambda s: s % (2 * GRID) >= GRID
    nowhere = (-1, 0)
    near = route(lambda s, c: (s + 1, 0) if c == 0 else (s - 1, 1))
    far_above = route(lambda s, c: (s + GRID, 0) if c == 0 else nowhere)
    far_below = route(
        lambda s, c: nowhere if c == 0 else (s - GRID, 0 if late(s - GRID) else 1)
    )

    size = block_sizes[0]
    positions = jnp.arange(extent)
    share = extent // chips
    strip = lax.dynamic_slice_in_dim(wavefunction[0], chip * share, share, 0)
    rows = chip * share + jnp.arange(share)
    strip = jnp.where((rows < size)[:, None] & (positions < size)[None, :], strip, 0)
    above_strip = lax.ppermute(strip, both, far_above)
    below_strip = lax.ppermute(strip, both, far_below)
    live = positions < size
    masked = jnp.where(live[:, None] & live[None, :], wavefunction[0], 0)
    near_one = lax.ppermute(masked, both, near)

    in_hbm = lambda a: pltpu.with_memory_space_constraint(a, pltpu.HBM)
    by_core = lambda a: in_hbm(a.reshape(a.shape[0], chips, CORES, step, extent))
    left, right = left_environment[:, 0], right_environment[:, 0]
    count = coupling.shape[0]
    lane = jnp.arange(2 * count + 2)
    mine = jnp.where(
        lane < count,
        jnp.pad(term_shift, (0, count + 2)).astype(jnp.float32),
        jnp.where(lane < 2 * count, jnp.pad(coupling, (count, 2)), size.astype(jnp.float32)),
    )
    mine = jnp.where(lane == 2 * count, parity.astype(jnp.float32), mine)
    right_other = lax.ppermute(right, "mpo", swap)
    left_other = lax.ppermute(left, "mpo", swap)
    other = lax.ppermute(mine, "mpo", swap)
    near_two = lax.ppermute(near_one, "mpo", swap)
    lefts = (by_core(left), by_core(left_other))
    rights = (in_hbm(right), in_hbm(right_other))
    shared = (mine, other, lefts, rights)

    far_strip = jnp.where(parity == 0, above_strip, below_strip)
    spread = jnp.broadcast_to(far_strip[None], (chips,) + far_strip.shape)
    far_one = lax.all_to_all(spread, "mpo", 0, 0, axis_index_groups=same_core)
    far_one = far_one.reshape(extent, extent)
    early = terms((masked, near_one, near_two), None, *shared)
    far_two = lax.ppermute(far_one, "mpo", swap)
    half = terms((far_one, far_two), early, *shared)
    half = half.astype(jnp.float16)
    pieces = lax.all_to_all(half, "mpo", 0, 0, axis_index_groups=same_core)
    pieces = pieces.astype(jnp.float32)
    factor = jnp.exp2(pieces[:, step : step + 1] - TOP)
    return jnp.sum(pieces[:, :step] * factor, axis=0)[None]


def solution(mesh):
    placed = (
        P("sector", None, None),
        P("mpo", "sector", None, None),
        P("mpo", "sector", None, None),
        P("mpo"),
        P("mpo"),
        P("sector"),
    )

    return jax.shard_map(
        per_device, mesh=mesh, in_specs=placed, out_specs=P("sector", "mpo", None), check_vma=False
    )
```
